32 devices in a mesh: region: 4 (over y, core), shard: 8 (over z, x).
Axes of the slice: x: 2, y: 2, z: 4, core: 2. Of those that a mesh axis runs over, the one named last changes fastest.
Arguments:
- fields: bfloat16 [32, 16384], P('shard', 'region'), may hold values from -6 to 6
- near_coef: bfloat16 [128, 3, 128, 128], P(('region', 'shard')), may hold values from -0.25 to 0.25
- far_coef: bfloat16 [128, 2, 128, 128], P(('region', 'shard')), may hold values from -0.25 to 0.25
- inv_factor: bfloat16 [128, 128, 128], P(('region', 'shard')), as said below
- near_block: int32 [128, 3], P(('region', 'shard')), may hold values from 0 to 3, as said below
- far_region: int32 [128, 2], P(('region', 'shard')), may hold values from 0 to 3, all different within a row; in each aligned block of 4 rows (0 to 3, 4 to 7, ...) at most 2 rows name the same one
- far_block: int32 [128, 2], P(('region', 'shard')), may hold values from 0 to 3
Outputs:
- whitened: bfloat16 [32, 16384], P('shard', 'region')
The draws below stay inside these ranges and needn't reach their ends.
Inputs may be any that keep to these rules, and one draw needn't show every extreme that they name: inv_factor[g] is upper triangular with a positive diagonal. `near_block`: row g lists 3 different indices of its own group of 4 blocks, never g % 4 itself. `far_region`: each row names 2 different regions; within the rows of one group of 4 blocks no region is named more than 2 times.
All inputs are finite; a program needn't handle non-finite values.
Results may differ from the reference program's by a relative error of at most 0.0049.
Values may be sent and summed in bfloat16 or wider, within the bound.
A program may use at most 64 MiB of HBM per device.

```python
import math
import jax
import jax.numpy as jnp
import numpy as np
from jax import lax

BLOCK = 128
FAR = 2
BLK_DEV = 4
NEAR = 3
SAMPLES = 32
NBLK = 128
NLOC = 16384
CAP = 2
N_REGION = 4
N_SHARD = 8


def draw_inv_factor(key, part):
    key_off, key_diag = jax.random.split(key)
    row_index = jnp.arange(BLOCK)[:, None]
    col_index = jnp.arange(BLOCK)[None, :]
    upper = col_index > row_index
    on_diag = col_index == row_index
    spread = 0.7 / math.sqrt(BLOCK)
    offdiag = jax.random.normal(key_off, (NBLK, BLOCK, BLOCK), jnp.float32) * spread
    diagonal = jax.random.uniform(key_diag, (NBLK, 1, BLOCK), jnp.float32, 0.5, 2.0)
    matrix = jnp.where(upper, offdiag, 0.0) + jnp.where(on_diag, diagonal, 0.0)
    return matrix.astype(jnp.bfloat16)


def draw_near_block(key, part):
    row_keys = jax.random.split(key, NBLK)
    orders = jax.vmap(lambda one_key: jax.random.permutation(one_key, BLK_DEV - 1))(row_keys)[:, :NEAR]
    own_index = (jnp.arange(NBLK, dtype=jnp.int32) % BLK_DEV)[:, None]
    return (orders + (orders >= own_index).astype(jnp.int32)).astype(jnp.int32)


def with_ends(values, stream_key, low, largest):
    spot = [jax.random.randint(jax.random.fold_in(stream_key, axis), (), 0, length) for axis, length in enumerate(values.shape)]
    widest = values.shape.index(max(values.shape))
    beside = spot[:widest] + [(spot[widest] + 1) % values.shape[widest]] + spot[widest + 1:]
    return values.at[tuple(spot)].set(low).at[tuple(beside)].set(largest)


def levels(own_key, dims, cuts, low, top_value):
    factor_of = 1.0
    for position, parts in cuts:
        draws = jax.random.uniform(jax.random.fold_in(jax.random.fold_in(own_key, 6), position), (parts,), jnp.float32, low / len(cuts), top_value / len(cuts))
        factor_of = factor_of * jnp.repeat(jnp.exp(draws), dims[position] // parts).reshape((-1,) + (1,) * (len(dims) - 1 - position))
    return factor_of


def deal_out(rng, own, number, rows, count, top, reach, skew):
    order = jax.random.permutation(rng, count)
    crowded, ordinary = shares(count, rows * top, reach, skew, True), shares(count, rows * top, reach, skew, False)
    places = jnp.arange(count)

    def named(lengths, turn):
        used = int((lengths > 0).sum())
        fixed = max(1, used // 4)
        shifted = fixed + (places - fixed + turn * (used - fixed)) % max(1, count - fixed)
        return jnp.zeros((count,), jnp.int32).at[order[jnp.where(places < fixed, places, shifted)]].set(jnp.asarray(lengths, jnp.int32))

    lengths = jnp.where(number % 4 == 0, named(crowded, number // 4), named(ordinary, number - number // 4 - 1))
    mixed = jax.random.permutation(jax.random.fold_in(own, 3), count)
    donor, taker = mixed[0:count // 2 * 2:2], mixed[1:count // 2 * 2:2]
    room = jnp.minimum(lengths[donor] - 1, reach - lengths[taker]) // 2
    room = jnp.where((donor == order[0]) | (taker == order[0]) | (lengths[taker] == 0), 0, jnp.maximum(room, 0))
    shifted = jax.random.randint(jax.random.fold_in(own, 4), (count // 2,), 0, 1 << 20) % (room + 1)
    lengths = lengths.at[donor].add(-shifted).at[taker].add(shifted)
    labels = jnp.searchsorted(jnp.cumsum(lengths), jnp.arange(rows * top), side="right").astype(jnp.int32)
    table = labels.reshape(top, rows).T
    table = table[jax.random.permutation(jax.random.fold_in(own, 1), rows)]
    turn = jax.random.randint(jax.random.fold_in(own, 2), (rows, 1), 0, top)
    return jnp.take_along_axis(table, (jnp.arange(top)[None, :] + turn) % top, axis=1)


def shares(number_of, total, limit, skew, full):
    portions = [(1 << 20) // math.isqrt(grade ** skew) + 1 for grade in range(1, number_of + 1)]
    largest = limit if full else min(limit, max(-(-total // number_of), total * portions[0] // sum(portions)))
    least = 1 if total - largest >= number_of - 1 else 0
    holding, surplus = [largest] + [least] * (number_of - 1), total - largest - least * (number_of - 1)
    while surplus > 0:
        free = [i for i in range(1, number_of) if holding[i] < largest] or [i for i in range(1, number_of) if holding[i] < limit]
        whole, budget = sum([portions[i] for i in free]), surplus
        for i in free:
            addition = min(limit - holding[i], max(1, budget * portions[i] // whole), surplus)
            holding[i] = holding[i] + addition
            surplus = surplus - addition
    return np.array(holding)


def normal_values(stream_key, extent, scale, bound, cuts=(), kind=jnp.bfloat16):
    level = levels(stream_key, extent, cuts, -0.22, 0.18) if cuts else 1.0
    values = jax.random.normal(stream_key, extent, jnp.float32) * scale * level
    return jnp.minimum(jnp.maximum(values, -bound), bound).astype(kind)


def setup_inputs(seed: int = 0) -> dict:
    key_list = jax.random.split(jax.random.key(seed), 8)
    fields = normal_values(key_list[0], (SAMPLES, NLOC), 1.0, 6.0, ((0, 8), (1, 4)))
    near_coef = normal_values(key_list[1], (NBLK, NEAR, BLOCK, BLOCK), (BLOCK * (NEAR + FAR)) ** -0.5, 0.25, ((0, 32),))
    far_coef = normal_values(key_list[2], (NBLK, FAR, BLOCK, BLOCK), (BLOCK * (NEAR + FAR)) ** -0.5, 0.25, ((0, 32),))
    inv_factor = draw_inv_factor(jax.random.fold_in(key_list[7], 71), 0)
    near_block = draw_near_block(jax.random.fold_in(key_list[7], 71), 0)
    far_region_keys = jax.random.split(jax.random.fold_in(key_list[5], 1), NBLK // BLK_DEV)
    far_region_turns = jax.random.permutation(jax.random.fold_in(key_list[5], 3), NBLK // BLK_DEV)
    far_region = jax.vmap(lambda own, number: deal_out(jax.random.fold_in(key_list[5], 2), own, number, BLK_DEV, N_REGION, FAR, CAP, 2))(far_region_keys, far_region_turns).reshape((NBLK, FAR))
    far_block = with_ends(jax.random.randint(key_list[6], (NBLK, FAR), 0, BLK_DEV), jax.random.fold_in(key_list[6], 1), 0, BLK_DEV - 1).astype(jnp.int32)
    return {"fields": fields, "near_coef": near_coef, "far_coef": far_coef, "inv_factor": inv_factor, "near_block": near_block, "far_region": far_region, "far_block": far_block}


def reference(fields, near_coef, far_coef, inv_factor, near_block, far_region, far_block):
    field_blocks = fields.reshape(SAMPLES, NBLK, BLOCK)
    block_ids = jnp.arange(NBLK, dtype=jnp.int32)
    group_of = block_ids // BLK_DEV
    near_ids = (group_of * BLK_DEV)[:, None] + near_block
    shard_of = group_of % N_SHARD
    far_ids = (far_region * N_SHARD + shard_of[:, None]) * BLK_DEV + far_block

    def one_group(group):
        start = (group * BLK_DEV).astype(jnp.int32)
        near_rows = lax.dynamic_slice_in_dim(near_ids, start, BLK_DEV, 0).reshape(-1).astype(jnp.int32)
        far_rows = lax.dynamic_slice_in_dim(far_ids, start, BLK_DEV, 0).reshape(-1).astype(jnp.int32)
        near_vals = jnp.take(field_blocks, near_rows, axis=1).reshape(SAMPLES, BLK_DEV, NEAR, BLOCK)
        far_vals = jnp.take(field_blocks, far_rows, axis=1).reshape(SAMPLES, BLK_DEV, FAR, BLOCK)
        own_vals = lax.dynamic_slice_in_dim(field_blocks, start, BLK_DEV, 1)
        near_here = lax.dynamic_slice_in_dim(near_coef, start, BLK_DEV, 0)
        far_here = lax.dynamic_slice_in_dim(far_coef, start, BLK_DEV, 0)
        factor_here = lax.dynamic_slice_in_dim(inv_factor, start, BLK_DEV, 0)
        cond_mean = jnp.einsum("sbjd,bjde->sbe", near_vals.astype(jnp.float32), near_here.astype(jnp.float32))
        cond_mean = cond_mean + jnp.einsum("sbjd,bjde->sbe", far_vals.astype(jnp.float32), far_here.astype(jnp.float32))
        residual = (own_vals.astype(jnp.float32) - cond_mean).astype(jnp.bfloat16)
        result = jnp.einsum("sbd,bde->sbe", residual.astype(jnp.float32), factor_here.astype(jnp.float32))
        return result.astype(jnp.bfloat16)

    grouped = lax.map(one_group, jnp.arange(NBLK // BLK_DEV, dtype=jnp.int32))
    return jnp.transpose(grouped, (1, 0, 2, 3)).reshape(SAMPLES, NLOC)
```

```python
import functools

import jax
import jax.numpy as jnp
from jax import lax
from jax.experimental import pallas as pl
from jax.experimental.pallas import tpu as pltpu
from jax.sharding import PartitionSpec as P

MESH = pl.DeviceIdType.MESH


def kernel(regions, shards, fields, near_coef, far_coef, inv_factor, near_block,
           far_region, far_block, out, own, near_land, far_land, near_x, near_w, far_w, inv_w, stage,
           load_sem, send_sem, recv_sem):
    rows = fields.shape[1]
    blocks, near, width = near_coef.shape[0], near_coef.shape[1], near_coef.shape[3]
    far = far_coef.shape[1]
    members = rows * shards
    r, s = lax.axis_index("region"), lax.axis_index("shard")

    def peer(dr, ds):
        return lax.rem(r + dr, regions), lax.rem(s + ds, shards)

    def each_shard(first, visit):
        if shards <= 8:
            for ds in range(first, shards):
                visit(ds)
        else:
            lax.fori_loop(first, shards, lambda ds, c: (visit(ds), c)[1], 0)

    barrier = pltpu.get_barrier_semaphore()
    for dr in range(regions):
        each_shard(1 if dr == 0 else 0, lambda ds: pl.semaphore_signal(
            barrier, inc=1, device_id=peer(dr, ds), device_id_type=MESH))

    loads = [pltpu.make_async_copy(a, b, load_sem.at[i]) for i, (a, b) in enumerate(
        [(fields, own), (near_coef, near_w), (far_coef, far_w), (inv_factor, inv_w)])]
    for load in loads:
        load.start()
    loads[0].wait()
    pl.semaphore_wait(barrier, regions * shards - 1)

    def group(index):
        return pl.ds(index * blocks, blocks)

    pltpu.make_async_copy(own.at[group(s)], near_land.at[:, s], recv_sem.at[0]).start()
    for dr in range(regions):
        stage_id = 0 if dr == 0 else 1
        place = far_land.at[group(regions - dr), s] if dr else near_land.at[:, s]

        def send(ds):
            rd, sd = peer(dr, ds)
            pltpu.make_async_remote_copy(
                src_ref=own.at[group(sd)], dst_ref=place,
                send_sem=send_sem.at[stage_id], recv_sem=recv_sem.at[stage_id],
                device_id=(rd, sd), device_id_type=MESH).start()

        each_shard(1 if dr == 0 else 0, send)

    def wait_for(ref, sem):
        pltpu.make_async_copy(ref, ref, sem).wait()

    wait_for(near_land, recv_sem.at[0])
    near_x[...] = near_land[...].reshape(blocks, members, width)
    far_land[:blocks] = near_land[...]
    loads[1].wait()
    means = []
    for b in range(blocks):
        x = jnp.concatenate([near_x[near_block[b, j]] for j in range(near)], axis=1)
        means.append(jnp.dot(x, near_w[b].reshape(near * width, width),
                             preferred_element_type=jnp.float32))
    loads[2].wait()
    loads[3].wait()
    others = far_land.at[pl.ds(blocks, (regions - 1) * blocks)]
    wait_for(others, recv_sem.at[1])
    for b in range(blocks):
        x = jnp.concatenate(
            [far_land[lax.rem(far_region[b, j] - r + regions, regions) * blocks
                      + far_block[b, j]].reshape(members, width) for j in range(far)], axis=1)
        mean = means[b] + jnp.dot(x, far_w[b].reshape(far * width, width),
                                  preferred_element_type=jnp.float32)
        residual = (near_x[b].astype(jnp.float32) - mean).astype(jnp.bfloat16)
        white = jnp.dot(residual, inv_w[b], preferred_element_type=jnp.float32)
        stage[:, b] = white.astype(jnp.bfloat16).reshape(shards, rows, width)

    pltpu.make_async_copy(stage.at[s], out.at[group(s)], recv_sem.at[2]).start()

    def give_back(ds):
        rd, sd = peer(0, ds)
        pltpu.make_async_remote_copy(
            src_ref=stage.at[sd], dst_ref=out.at[group(s)],
            send_sem=send_sem.at[2], recv_sem=recv_sem.at[2],
            device_id=(rd, sd), device_id_type=MESH).start()

    each_shard(1, give_back)
    wait_for(near_land.at[:, pl.ds(0, shards - 1)], send_sem.at[0])
    wait_for(others, send_sem.at[1])
    wait_for(stage.at[pl.ds(0, shards - 1)], send_sem.at[2])
    wait_for(out, recv_sem.at[2])


def body(fields, near_coef, far_coef, inv_factor, near_block, far_region, far_block):
    shards, regions = lax.axis_size("shard"), lax.axis_size("region")
    rows, columns = fields.shape
    blocks, width = near_coef.shape[0], near_coef.shape[3]
    tiles = columns // width
    tiled = jnp.transpose(fields.reshape(rows, tiles, width), (1, 0, 2))
    hbm = pl.BlockSpec(memory_space=pl.ANY)
    smem = pl.BlockSpec(memory_space=pltpu.SMEM)
    white = pl.pallas_call(
        functools.partial(kernel, regions, shards),
        out_shape=jax.ShapeDtypeStruct(tiled.shape, jnp.bfloat16),
        in_specs=[hbm] * 4 + [smem] * 3,
        out_specs=pl.BlockSpec(memory_space=pltpu.VMEM),
        scratch_shapes=[
            pltpu.VMEM(tiled.shape, jnp.bfloat16),
            pltpu.VMEM((blocks, shards, rows, width), jnp.bfloat16),
            pltpu.VMEM((regions * blocks, shards, rows, width), jnp.bfloat16),
            pltpu.VMEM((blocks, shards * rows, width), jnp.bfloat16),
            pltpu.VMEM(near_coef.shape, jnp.bfloat16),
            pltpu.VMEM(far_coef.shape, jnp.bfloat16),
            pltpu.VMEM(inv_factor.shape, jnp.bfloat16),
            pltpu.VMEM((shards, blocks, rows, width), jnp.bfloat16),
            pltpu.SemaphoreType.DMA((4,)),
            pltpu.SemaphoreType.DMA((3,)),
            pltpu.SemaphoreType.DMA((3,)),
        ],
        compiler_params=pltpu.CompilerParams(collective_id=0, has_side_effects=True),
    )(tiled, near_coef, far_coef, inv_factor, near_block, far_region, far_block)
    return jnp.transpose(white, (1, 0, 2)).reshape(rows, columns)


def solution(mesh):
    return jax.shard_map(
        body,
        mesh=mesh,
        in_specs=(
            P("shard", "region"),
            P(("region", "shard"), None, None, None),
            P(("region", "shard"), None, None, None),
            P(("region", "shard"), None, None),
            P(("region", "shard"), None),
            P(("region", "shard"), None),
            P(("region", "shard"), None),
        ),
        out_specs=P("shard", "region"),
        check_vma=False,
    )
```

```python
import functools

import jax
import jax.numpy as jnp
from jax import lax
from jax.experimental import pallas as pl
from jax.experimental.pallas import tpu as pltpu
from jax.sharding import PartitionSpec as P

MESH = pl.DeviceIdType.MESH


def kernel(regions, shards, fields, near_coef, far_coef, inv_factor, near_list,
           region_list, block_list, out, own, near_land, far_land, near_x, near_w,
           far_w, inv_w, stage, near_block, far_region, far_block, load_sem, send_sem, recv_sem):
    rows = fields.shape[1]
    blocks, near, width = near_coef.shape[0], near_coef.shape[1], near_coef.shape[3]
    far = far_coef.shape[1]
    members = rows * shards
    r, s = lax.axis_index("region"), lax.axis_index("shard")

    def peer(dr, ds):
        return lax.rem(r + dr, regions), lax.rem(s + ds, shards)

    def each_shard(first, visit):
        if shards <= 8:
            for ds in range(first, shards):
                visit(ds)
        else:
            lax.fori_loop(first, shards, lambda ds, c: (visit(ds), c)[1], 0)

    barrier = pltpu.get_barrier_semaphore()

    def greet(dr, ds):
        pl.semaphore_signal(barrier, inc=1, device_id=peer(dr, ds), device_id_type=MESH)

    each_shard(1, lambda ds: greet(0, ds))
    for dr in range(1, regions):
        greet(dr, 0)

    loads = [pltpu.make_async_copy(a, b, load_sem.at[i]) for i, (a, b) in enumerate(
        [(fields, own), (near_list, near_block), (region_list, far_region),
         (block_list, far_block), (near_coef, near_w), (far_coef, far_w),
         (inv_factor, inv_w)])]
    for load in loads:
        load.start()
    loads[0].wait()
    pl.semaphore_wait(barrier, shards + regions - 2)

    def group(index):
        return pl.ds(index * blocks, blocks)

    pltpu.make_async_copy(own.at[group(s)], near_land.at[:, s], recv_sem.at[0]).start()

    def gather(ds):
        rd, sd = peer(0, ds)
        pltpu.make_async_remote_copy(
            src_ref=own.at[group(sd)], dst_ref=near_land.at[:, s],
            send_sem=send_sem.at[0], recv_sem=recv_sem.at[0],
            device_id=(rd, sd), device_id_type=MESH).start()

    each_shard(1, gather)

    def wait_for(ref, sem):
        pltpu.make_async_copy(ref, ref, sem).wait()

    wait_for(near_land, recv_sem.at[0])
    for dr in range(1, regions):
        rd, sd = peer(dr, 0)
        pltpu.make_async_remote_copy(
            src_ref=near_land, dst_ref=far_land.at[group(regions - dr)],
            send_sem=send_sem.at[1], recv_sem=recv_sem.at[1],
            device_id=(rd, sd), device_id_type=MESH).start()
    near_x[...] = near_land[...].reshape(blocks, members, width)
    far_land[:blocks] = near_land[...]
    for load in loads[1:5]:
        load.wait()
    means = []
    for b in range(blocks):
        x = jnp.concatenate([near_x[near_block[b, j]] for j in range(near)], axis=1)
        means.append(jnp.dot(x, near_w[b].reshape(near * width, width),
                             preferred_element_type=jnp.float32))
    loads[5].wait()
    loads[6].wait()
    others = far_land.at[pl.ds(blocks, (regions - 1) * blocks)]
    wait_for(others, recv_sem.at[1])
    for b in range(blocks):
        x = jnp.concatenate(
            [far_land[lax.rem(far_region[j, b] - r + regions, regions) * blocks
                      + far_block[j, b]].reshape(members, width) for j in range(far)], axis=1)
        mean = means[b] + jnp.dot(x, far_w[b].reshape(far * width, width),
                                  preferred_element_type=jnp.float32)
        residual = (near_x[b].astype(jnp.float32) - mean).astype(jnp.bfloat16)
        white = jnp.dot(residual, inv_w[b], preferred_element_type=jnp.float32)
        stage[:, b] = white.astype(jnp.bfloat16).reshape(shards, rows, width)

    pltpu.make_async_copy(stage.at[s], out.at[group(s)], recv_sem.at[2]).start()

    def give_back(ds):
        rd, sd = peer(0, ds)
        pltpu.make_async_remote_copy(
            src_ref=stage.at[sd], dst_ref=out.at[group(s)],
            send_sem=send_sem.at[2], recv_sem=recv_sem.at[2],
            device_id=(rd, sd), device_id_type=MESH).start()

    each_shard(1, give_back)
    wait_for(near_land.at[:, pl.ds(0, shards - 1)], send_sem.at[0])
    wait_for(others, send_sem.at[1])
    wait_for(stage.at[pl.ds(0, shards - 1)], send_sem.at[2])
    wait_for(out, recv_sem.at[2])


def body(fields, near_coef, far_coef, inv_factor, near_block, far_region, far_block):
    shards, regions = lax.axis_size("shard"), lax.axis_size("region")
    rows, columns = fields.shape
    blocks, width = near_coef.shape[0], near_coef.shape[3]
    tiles = columns // width
    tiled = jnp.transpose(fields.reshape(rows, tiles, width), (1, 0, 2))
    hbm = pl.BlockSpec(memory_space=pl.ANY)
    white = pl.pallas_call(
        functools.partial(kernel, regions, shards),
        out_shape=pltpu.VMEM(tiled.shape, jnp.bfloat16),
        in_specs=[hbm] * 7,
        out_specs=pl.BlockSpec(memory_space=pltpu.VMEM),
        scratch_shapes=[
            pltpu.VMEM(tiled.shape, jnp.bfloat16),
            pltpu.VMEM((blocks, shards, rows, width), jnp.bfloat16),
            pltpu.VMEM((regions * blocks, shards, rows, width), jnp.bfloat16),
            pltpu.VMEM((blocks, shards * rows, width), jnp.bfloat16),
            pltpu.VMEM(near_coef.shape, jnp.bfloat16),
            pltpu.VMEM(far_coef.shape, jnp.bfloat16),
            pltpu.VMEM(inv_factor.shape, jnp.bfloat16),
            pltpu.VMEM((shards, blocks, rows, width), jnp.bfloat16),
            pltpu.SMEM(near_block.shape, jnp.int32),
            pltpu.SMEM(far_region.T.shape, jnp.int32),
            pltpu.SMEM(far_block.T.shape, jnp.int32),
            pltpu.SemaphoreType.DMA((7,)),
            pltpu.SemaphoreType.DMA((3,)),
            pltpu.SemaphoreType.DMA((3,)),
        ],
        compiler_params=pltpu.CompilerParams(collective_id=0, has_side_effects=True),
    )(tiled, near_coef, far_coef, inv_factor, near_block, far_region.T, far_block.T)
    return jnp.transpose(white, (1, 0, 2)).reshape(rows, columns)


def solution(mesh):
    return jax.shard_map(
        body,
        mesh=mesh,
        in_specs=(
            P("shard", "region"),
            P(("region", "shard"), None, None, None),
            P(("region", "shard"), None, None, None),
            P(("region", "shard"), None, None),
            P(("region", "shard"), None),
            P(("region", "shard"), None),
            P(("region", "shard"), None),
        ),
        out_specs=P("shard", "region"),
        check_vma=False,
    )
```

```python
import functools

import jax
import jax.numpy as jnp
from jax import lax
from jax.experimental import pallas as pl
from jax.experimental.pallas import tpu as pltpu
from jax.sharding import PartitionSpec as P

WAVES = 4
DIRECT = (1, 2, 3)
MESH = pl.DeviceIdType.MESH


def kernel(regions, shards, fields, near_coef, far_coef, inv_factor, near_list,
           region_list, block_list, out, own, near_land, far_land, near_x, near_w,
           far_w, inv_w, stage, near_block, far_region, far_block, load_sem, send_sem, recv_sem, near_sem):
    rows = fields.shape[1]
    blocks, near, width = near_coef.shape[0], near_coef.shape[1], near_coef.shape[3]
    far = far_coef.shape[1]
    members = rows * shards
    r, s = lax.axis_index("region"), lax.axis_index("shard")

    def peer(dr, ds):
        return lax.rem(r + dr, regions), lax.rem(s + ds, shards)

    run = shards // WAVES

    def flipped(q, w):
        for bit in (1, 2):
            if w & bit:
                q = q + bit * (1 - 2 * lax.rem(lax.div(q, bit), 2))
        return q

    mine = lax.div(s, run)

    def partner(w, i):
        return flipped(mine, w) * run + lax.rem(lax.rem(s, run) + i, run)

    barrier = pltpu.get_barrier_semaphore()
    met = 0
    for w in range(WAVES):
        for i in range(run):
            for dr in range(regions):
                if (w or i) if dr == 0 else (w in DIRECT or (w == 0 and i == 0)):
                    met += 1
                    pl.semaphore_signal(
                        barrier, inc=1, device_id=(lax.rem(r + dr, regions), partner(w, i)),
                        device_id_type=MESH)

    loads = [pltpu.make_async_copy(a, b, load_sem.at[i]) for i, (a, b) in enumerate(
        [(fields, own), (near_list, near_block), (region_list, far_region),
         (block_list, far_block), (near_coef, near_w), (far_coef, far_w),
         (inv_factor, inv_w)])]
    for load in loads:
        load.start()
    loads[0].wait()
    pl.semaphore_wait(barrier, met)

    def group(index):
        return pl.ds(index * blocks, blocks)

    def visit(w, i, dr):
        sd = partner(w, i)
        pltpu.make_async_remote_copy(
            src_ref=own.at[group(sd)],
            dst_ref=far_land.at[group(regions - dr), s] if dr else near_land.at[:, s],
            send_sem=send_sem.at[1 if dr else 0],
            recv_sem=recv_sem.at[1] if dr else near_sem.at[w],
            device_id=(lax.rem(r + dr, regions), sd), device_id_type=MESH).start()

    pltpu.make_async_copy(own.at[group(s)], near_land.at[:, s], near_sem.at[0]).start()
    for w in reversed(range(WAVES)):
        for i in range(1 if w == 0 else 0, run):
            visit(w, i, 0)
    for w in reversed(DIRECT):
        for i in range(run):
            for dr in range(1, regions):
                visit(w, i, dr)

    def wait_for(ref, sem):
        pltpu.make_async_copy(ref, ref, sem).wait()

    for w in range(WAVES):
        part = pl.ds(flipped(mine, w) * run, run)
        wait_for(near_land.at[:, part], near_sem.at[w])
        for dr in range(1, regions if w not in DIRECT else 1):
            pltpu.make_async_remote_copy(
                src_ref=near_land.at[:, part],
                dst_ref=far_land.at[group(regions - dr), part],
                send_sem=send_sem.at[1], recv_sem=recv_sem.at[1],
                device_id=peer(dr, 0), device_id_type=MESH).start()
    near_x[...] = near_land[...].reshape(blocks, members, width)
    far_land[:blocks] = near_land[...]
    for load in loads[1:5]:
        load.wait()
    means = []
    for b in range(blocks):
        x = jnp.concatenate([near_x[near_block[b, j]] for j in range(near)], axis=1)
        means.append(jnp.dot(x, near_w[b].reshape(near * width, width),
                             preferred_element_type=jnp.float32))
    loads[5].wait()
    loads[6].wait()
    others = far_land.at[pl.ds(blocks, (regions - 1) * blocks)]
    wait_for(others, recv_sem.at[1])
    for b in range(blocks):
        x = jnp.concatenate(
            [far_land[lax.rem(far_region[j, b] - r + regions, regions) * blocks
                      + far_block[j, b]].reshape(members, width) for j in range(far)], axis=1)
        mean = means[b] + jnp.dot(x, far_w[b].reshape(far * width, width),
                                  preferred_element_type=jnp.float32)
        residual = (near_x[b].astype(jnp.float32) - mean).astype(jnp.bfloat16)
        white = jnp.dot(residual, inv_w[b], preferred_element_type=jnp.float32)
        stage[:, b] = white.astype(jnp.bfloat16).reshape(shards, rows, width)

    pltpu.make_async_copy(stage.at[s], out.at[group(s)], recv_sem.at[2]).start()

    def give_back(sd):
        pltpu.make_async_remote_copy(
            src_ref=stage.at[sd], dst_ref=out.at[group(s)],
            send_sem=send_sem.at[2], recv_sem=recv_sem.at[2],
            device_id=(r, sd), device_id_type=MESH).start()

    for w in reversed(range(WAVES)):
        for i in range(1 if w == 0 else 0, run):
            give_back(partner(w, i))

    wait_for(near_land.at[:, pl.ds(0, shards - 1)], send_sem.at[0])
    wait_for(others, send_sem.at[1])
    wait_for(stage.at[pl.ds(0, shards - 1)], send_sem.at[2])
    wait_for(out, recv_sem.at[2])


def body(fields, near_coef, far_coef, inv_factor, near_block, far_region, far_block):
    shards, regions = lax.axis_size("shard"), lax.axis_size("region")
    rows, columns = fields.shape
    blocks, width = near_coef.shape[0], near_coef.shape[3]
    tiles = columns // width
    tiled = jnp.transpose(fields.reshape(rows, tiles, width), (1, 0, 2))
    hbm = pl.BlockSpec(memory_space=pl.ANY)
    white = pl.pallas_call(
        functools.partial(kernel, regions, shards),
        out_shape=pltpu.VMEM(tiled.shape, jnp.bfloat16),
        in_specs=[hbm] * 7,
        out_specs=pl.BlockSpec(memory_space=pltpu.VMEM),
        scratch_shapes=[
            pltpu.VMEM(tiled.shape, jnp.bfloat16),
            pltpu.VMEM((blocks, shards, rows, width), jnp.bfloat16),
            pltpu.VMEM((regions * blocks, shards, rows, width), jnp.bfloat16),
            pltpu.VMEM((blocks, shards * rows, width), jnp.bfloat16),
            pltpu.VMEM(near_coef.shape, jnp.bfloat16),
            pltpu.VMEM(far_coef.shape, jnp.bfloat16),
            pltpu.VMEM(inv_factor.shape, jnp.bfloat16),
            pltpu.VMEM((shards, blocks, rows, width), jnp.bfloat16),
            pltpu.SMEM(near_block.shape, jnp.int32),
            pltpu.SMEM(far_region.T.shape, jnp.int32),
            pltpu.SMEM(far_block.T.shape, jnp.int32),
            pltpu.SemaphoreType.DMA((7,)),
            pltpu.SemaphoreType.DMA((3,)),
            pltpu.SemaphoreType.DMA((3,)),
            pltpu.SemaphoreType.DMA((WAVES,)),
        ],
        compiler_params=pltpu.CompilerParams(collective_id=0, has_side_effects=True),
    )(tiled, near_coef, far_coef, inv_factor, near_block, far_region.T, far_block.T)
    return jnp.transpose(white, (1, 0, 2)).reshape(rows, columns)


def solution(mesh):
    return jax.shard_map(
        body,
        mesh=mesh,
        in_specs=(
            P("shard", "region"),
            P(("region", "shard"), None, None, None),
            P(("region", "shard"), None, None, None),
            P(("region", "shard"), None, None),
            P(("region", "shard"), None),
            P(("region", "shard"), None),
            P(("region", "shard"), None),
        ),
        out_specs=P("shard", "region"),
        check_vma=False,
    )
```

```python
import functools

import jax
import jax.numpy as jnp
from jax import lax
from jax.experimental import pallas as pl
from jax.experimental.pallas import tpu as pltpu
from jax.sharding import PartitionSpec as P

WAVES = 8
DIRECT = (2, 3, 4, 5, 6, 7)
MESH = pl.DeviceIdType.MESH


def kernel(regions, shards, fields, near_coef, far_coef, inv_factor, near_list,
           region_list, block_list, out, own, near_land, far_land, near_x, near_w,
           far_w, inv_w, stage, near_block, far_region, far_block, load_sem, send_sem, recv_sem, near_sem):
    rows = fields.shape[1]
    blocks, near, width = near_coef.shape[0], near_coef.shape[1], near_coef.shape[3]
    far = far_coef.shape[1]
    members = rows * shards
    r, s = lax.axis_index("region"), lax.axis_index("shard")

    def peer(dr, ds):
        return lax.rem(r + dr, regions), lax.rem(s + ds, shards)

    run = shards // WAVES

    def flipped(q, w):
        for bit in (1, 2, 4):
            if w & bit:
                q = q + bit * (1 - 2 * lax.rem(lax.div(q, bit), 2))
        return q

    mine = lax.div(s, run)

    def partner(w, i):
        return flipped(mine, w) * run + lax.rem(lax.rem(s, run) + i, run)

    barrier = pltpu.get_barrier_semaphore()
    met = 0
    for w in range(WAVES):
        for i in range(run):
            for dr in range(regions):
                if (w or i) if dr == 0 else (w in DIRECT or (w == 0 and i == 0)):
                    met += 1
                    pl.semaphore_signal(
                        barrier, inc=1, device_id=(lax.rem(r + dr, regions), partner(w, i)),
                        device_id_type=MESH)

    loads = [pltpu.make_async_copy(a, b, load_sem.at[i]) for i, (a, b) in enumerate(
        [(fields, own), (near_list, near_block), (region_list, far_region),
         (block_list, far_block), (near_coef, near_w), (far_coef, far_w),
         (inv_factor, inv_w)])]
    for load in loads:
        load.start()
    loads[0].wait()
    pl.semaphore_wait(barrier, met)

    def group(index):
        return pl.ds(index * blocks, blocks)

    def visit(w, i, dr):
        sd = partner(w, i)
        pltpu.make_async_remote_copy(
            src_ref=own.at[group(sd)],
            dst_ref=far_land.at[group(regions - dr), s] if dr else near_land.at[:, s],
            send_sem=send_sem.at[1 if dr else 0],
            recv_sem=recv_sem.at[1] if dr else near_sem.at[w],
            device_id=(lax.rem(r + dr, regions), sd), device_id_type=MESH).start()

    pltpu.make_async_copy(own.at[group(s)], near_land.at[:, s], near_sem.at[0]).start()
    for w in reversed(range(WAVES)):
        for i in range(1 if w == 0 else 0, run):
            visit(w, i, 0)
    for w in reversed(DIRECT):
        for i in range(run):
            for dr in range(1, regions):
                visit(w, i, dr)

    def wait_for(ref, sem):
        pltpu.make_async_copy(ref, ref, sem).wait()

    for w in range(WAVES):
        part = pl.ds(flipped(mine, w) * run, run)
        wait_for(near_land.at[:, part], near_sem.at[w])
        for dr in range(1, regions if w not in DIRECT else 1):
            pltpu.make_async_remote_copy(
                src_ref=near_land.at[:, part],
                dst_ref=far_land.at[group(regions - dr), part],
                send_sem=send_sem.at[1], recv_sem=recv_sem.at[1],
                device_id=peer(dr, 0), device_id_type=MESH).start()
    near_x[...] = near_land[...].reshape(blocks, members, width)
    far_land[:blocks] = near_land[...]
    for load in loads[1:5]:
        load.wait()
    means = []
    for b in range(blocks):
        x = jnp.concatenate([near_x[near_block[b, j]] for j in range(near)], axis=1)
        means.append(jnp.dot(x, near_w[b].reshape(near * width, width),
                             preferred_element_type=jnp.float32))
    loads[5].wait()
    loads[6].wait()
    others = far_land.at[pl.ds(blocks, (regions - 1) * blocks)]
    wait_for(others, recv_sem.at[1])
    for b in range(blocks):
        x = jnp.concatenate(
            [far_land[lax.rem(far_region[j, b] - r + regions, regions) * blocks
                      + far_block[j, b]].reshape(members, width) for j in range(far)], axis=1)
        mean = means[b] + jnp.dot(x, far_w[b].reshape(far * width, width),
                                  preferred_element_type=jnp.float32)
        residual = (near_x[b].astype(jnp.float32) - mean).astype(jnp.bfloat16)
        white = jnp.dot(residual, inv_w[b], preferred_element_type=jnp.float32)
        stage[:, b] = white.astype(jnp.bfloat16).reshape(shards, rows, width)

    pltpu.make_async_copy(stage.at[s], out.at[group(s)], recv_sem.at[2]).start()

    def give_back(sd):
        pltpu.make_async_remote_copy(
            src_ref=stage.at[sd], dst_ref=out.at[group(s)],
            send_sem=send_sem.at[2], recv_sem=recv_sem.at[2],
            device_id=(r, sd), device_id_type=MESH).start()

    for w in reversed(range(WAVES)):
        for i in range(1 if w == 0 else 0, run):
            give_back(partner(w, i))

    wait_for(near_land.at[:, pl.ds(0, shards - 1)], send_sem.at[0])
    wait_for(others, send_sem.at[1])
    wait_for(stage.at[pl.ds(0, shards - 1)], send_sem.at[2])
    wait_for(out, recv_sem.at[2])


def body(fields, near_coef, far_coef, inv_factor, near_block, far_region, far_block):
    shards, regions = lax.axis_size("shard"), lax.axis_size("region")
    rows, columns = fields.shape
    blocks, width = near_coef.shape[0], near_coef.shape[3]
    tiles = columns // width
    tiled = jnp.transpose(fields.reshape(rows, tiles, width), (1, 0, 2))
    hbm = pl.BlockSpec(memory_space=pl.ANY)
    white = pl.pallas_call(
        functools.partial(kernel, regions, shards),
        out_shape=pltpu.VMEM(tiled.shape, jnp.bfloat16),
        in_specs=[hbm] * 7,
        out_specs=pl.BlockSpec(memory_space=pltpu.VMEM),
        scratch_shapes=[
            pltpu.VMEM(tiled.shape, jnp.bfloat16),
            pltpu.VMEM((blocks, shards, rows, width), jnp.bfloat16),
            pltpu.VMEM((regions * blocks, shards, rows, width), jnp.bfloat16),
            pltpu.VMEM((blocks, shards * rows, width), jnp.bfloat16),
            pltpu.VMEM(near_coef.shape, jnp.bfloat16),
            pltpu.VMEM(far_coef.shape, jnp.bfloat16),
            pltpu.VMEM(inv_factor.shape, jnp.bfloat16),
            pltpu.VMEM((shards, blocks, rows, width), jnp.bfloat16),
            pltpu.SMEM(near_block.shape, jnp.int32),
            pltpu.SMEM(far_region.T.shape, jnp.int32),
            pltpu.SMEM(far_block.T.shape, jnp.int32),
            pltpu.SemaphoreType.DMA((7,)),
            pltpu.SemaphoreType.DMA((3,)),
            pltpu.SemaphoreType.DMA((3,)),
            pltpu.SemaphoreType.DMA((WAVES,)),
        ],
        compiler_params=pltpu.CompilerParams(collective_id=0, has_side_effects=True),
    )(tiled, near_coef, far_coef, inv_factor, near_block, far_region.T, far_block.T)
    return jnp.transpose(white, (1, 0, 2)).reshape(rows, columns)


def solution(mesh):
    return jax.shard_map(
        body,
        mesh=mesh,
        in_specs=(
            P("shard", "region"),
            P(("region", "shard"), None, None, None),
            P(("region", "shard"), None, None, None),
            P(("region", "shard"), None, None),
            P(("region", "shard"), None),
            P(("region", "shard"), None),
            P(("region", "shard"), None),
        ),
        out_specs=P("shard", "region"),
        check_vma=False,
    )
```
